512 devices in a mesh: query: 4 (over x), corpus: 16 (over z), cent: 8 (over y, core).
Axes of the slice: x: 4, y: 4, z: 16, core: 2. Of those that a mesh axis runs over, the one named last changes fastest.
Arguments:
- request_term_embeds: bfloat16 [64, 32, 128], P('query'), may hold values from -6 to 6
- cluster_means: bfloat16 [65536, 128], P(('corpus', 'cent')), may hold values from -0.5 to 0.5
- cluster_shard_number: int32 [8192, 64, 1], P(('corpus', 'cent')), may hold values from 0 to 127; in each aligned block of 4096 rows (0 to 4095, 4096 to 8191, ..., all dimensions but the last counted through in order) at most 64 rows name the same one
- cluster_entry_within: int32 [8192, 64], P(('corpus', 'cent')), may hold values from 0 to 511
- quantized_error_words: int32 [8192, 1024], P(('corpus', 'cent')), may hold values from 0 to 65535
- quantized_error_amounts: float32 [4], replicated, may hold values from -0.2 to 0.2
- keeper_document_position: int32 [64, 128, 16], P('query', ('corpus', 'cent')), may hold values from 0 to 63, as said below
- active_keeper_tally: int32 [64, 128], P('query', ('corpus', 'cent')), may hold values from 2 to 16, as said below
Outputs:
- approx_scores: float32 [64, 128, 16], P('query', ('corpus', 'cent'))
- exact_scores: float32 [64, 128, 16], P('query', ('corpus', 'cent'))
- best_scores: float32 [64, 8], P('query')
The draws below stay inside these ranges and needn't reach their ends.
Inputs may be any that keep to these rules, and one draw needn't show every extreme that they name: `cluster_shard_number`: among the 4096 tokens of the passages of one device (aligned blocks of rows), no block value is named by more than 64 tokens; some value is named by exactly 64. `keeper_document_position`: the 16 slots of one query on one shard name different passages. `active_keeper_tally`: every query has 16 live slots on some passage shard.
All inputs are finite; a program needn't handle non-finite values.
Results may differ from the reference program's by a relative error of at most 0.00033.
Values may be sent and summed in bfloat16 or wider, within the bound.
A program may use at most 64 MiB of HBM per device.

```python
import math
import jax
import jax.numpy as jnp
import numpy as np
from jax import lax

DIM = 128
QTOK = 32
DOC = 64
DOCS_PER_CHIP = 64
CENT_DEV = 512
KEEPER_SEATS = 16
TOPK = 8
SHARD_TOTAL = 128
CAP = 64
REQUEST_TOTAL = 64
PASSAGES = 8192
CENTROIDS = 65536


def draw_keeper_document_position(key, part):
    row_keys = jax.random.split(jax.random.fold_in(key, 21), REQUEST_TOTAL * SHARD_TOTAL)

    def one_row(random_state_per_line):
        return jax.random.permutation(random_state_per_line, DOCS_PER_CHIP)[:KEEPER_SEATS]
    chosen_entries = jax.vmap(one_row)(row_keys)
    return chosen_entries.reshape(REQUEST_TOTAL, SHARD_TOTAL, KEEPER_SEATS).astype(jnp.int32)


def draw_active_keeper_tally(key, part):
    seed_random_state = jax.random.fold_in(key, 11)
    pick_key = jax.random.fold_in(key, 12)
    tallies_per_shard = jax.random.randint(seed_random_state, (REQUEST_TOTAL, SHARD_TOTAL), 2, KEEPER_SEATS + 1, dtype=jnp.int32)
    complete_lookup = jax.random.randint(pick_key, (REQUEST_TOTAL, 1), 0, SHARD_TOTAL, dtype=jnp.int32)
    entry_positions = jnp.arange(SHARD_TOTAL, dtype=jnp.int32)[None, :]
    return jnp.where(entry_positions == complete_lookup, KEEPER_SEATS, tallies_per_shard).astype(jnp.int32)


def with_ends(values, rng, low, top_value):
    longest = values.shape.index(max(values.shape))
    spots = []
    for shift in (0, 1):
        where = [jax.random.randint(jax.random.fold_in(rng, axis), (), 0, length) for axis, length in enumerate(values.shape)]
        where[longest] = (where[longest] + shift) % values.shape[longest]
        spots.append(tuple(where))
    return values.at[spots[0]].set(low).at[spots[1]].set(top_value)


def block_scale(key, dims, pieces, smallest, largest):
    factor_of = 1.0
    for dim, parts in pieces:
        steps = jax.random.uniform(jax.random.fold_in(jax.random.fold_in(key, 6), dim), (parts,), jnp.float32, smallest / len(pieces), largest / len(pieces))
        factor_of = factor_of * jnp.repeat(jnp.exp(steps), dims[dim] // parts).reshape((-1,) + (1,) * (len(dims) - 1 - dim))
    return factor_of


def deal_out(own_key, own, number, rows, number_of, top, bound, lean):
    sequence = jax.random.permutation(own_key, number_of)
    packed, common = portions_of(number_of, rows * top, bound, lean, True), portions_of(number_of, rows * top, bound, lean, False)
    places = jnp.arange(number_of)

    def named(sizes, offset_by):
        used = int((sizes > 0).sum())
        fixed = max(1, used // 4)
        shifted = fixed + (places - fixed + offset_by * (used - fixed)) % max(1, number_of - fixed)
        return jnp.zeros((number_of,), jnp.int32).at[sequence[jnp.where(places < fixed, places, shifted)]].set(jnp.asarray(sizes, jnp.int32))

    sizes = jnp.where(number % 4 == 0, named(packed, number // 4), named(common, number - number // 4 - 1))
    mixed = jax.random.permutation(jax.random.fold_in(own, 3), number_of)
    donor, receiver = mixed[0:number_of // 2 * 2:2], mixed[1:number_of // 2 * 2:2]
    room = jnp.minimum(sizes[donor] - 1, bound - sizes[receiver]) // 2
    room = jnp.where((donor == sequence[0]) | (receiver == sequence[0]) | (sizes[receiver] == 0), 0, jnp.maximum(room, 0))
    shifted = jax.random.randint(jax.random.fold_in(own, 4), (number_of // 2,), 0, 1 << 20) % (room + 1)
    sizes = sizes.at[donor].add(-shifted).at[receiver].add(shifted)
    items = jnp.searchsorted(jnp.cumsum(sizes), jnp.arange(rows * top), side="right").astype(jnp.int32)
    table = items.reshape(top, rows).T
    table = table[jax.random.permutation(jax.random.fold_in(own, 1), rows)]
    offset_by = jax.random.randint(jax.random.fold_in(own, 2), (rows, 1), 0, top)
    return jnp.take_along_axis(table, (jnp.arange(top)[None, :] + offset_by) % top, axis=1)


def portions_of(amount, total, reach, lean, full):
    portions = [(1 << 20) // math.isqrt(standing ** lean) + 1 for standing in range(1, amount + 1)]
    largest = reach if full else min(reach, max(-(-total // amount), total * portions[0] // sum(portions)))
    least = 1 if total - largest >= amount - 1 else 0
    counts, spare = [largest] + [least] * (amount - 1), total - largest - least * (amount - 1)
    while spare > 0:
        candidates = [i for i in range(1, amount) if counts[i] < largest] or [i for i in range(1, amount) if counts[i] < reach]
        whole, budget = sum([portions[i] for i in candidates]), spare
        for i in candidates:
            addition = min(reach - counts[i], max(1, budget * portions[i] // whole), spare)
            counts[i] = counts[i] + addition
            spare = spare - addition
    return np.array(counts)


def normal_values(key, extent, width, bound, shards=(), kind=jnp.bfloat16):
    entries = width * jax.random.normal(key, extent, jnp.float32)
    if shards:
        entries = entries * block_scale(key, extent, shards, -0.22, 0.18)
    return jnp.clip(entries, -bound, bound).astype(kind)


def setup_inputs(seed: int = 0) -> dict:
    keys = jax.random.split(jax.random.key(seed), 9)
    request_term_embeds = normal_values(keys[0], (REQUEST_TOTAL, QTOK, DIM), 1.0, 6.0, ((0, 4),))
    cluster_means = normal_values(keys[1], (CENTROIDS, DIM), DIM ** -0.5, 0.5, ((0, 128),))
    cluster_shard_number_keys = jax.random.split(jax.random.fold_in(keys[2], 1), PASSAGES * DOC // (DOCS_PER_CHIP * DOC))
    cluster_shard_number_turns = jax.random.permutation(jax.random.fold_in(keys[2], 3), PASSAGES * DOC // (DOCS_PER_CHIP * DOC))
    cluster_shard_number = jax.vmap(lambda own, number: deal_out(jax.random.fold_in(keys[2], 2), own, number, DOCS_PER_CHIP * DOC, SHARD_TOTAL, 1, CAP, 2))(cluster_shard_number_keys, cluster_shard_number_turns).reshape((PASSAGES, DOC, 1))
    cluster_entry_within = with_ends(jax.random.randint(keys[3], (PASSAGES, DOC), 0, CENT_DEV), jax.random.fold_in(keys[3], 1), 0, CENT_DEV - 1).astype(jnp.int32)
    quantized_error_words = with_ends(jax.random.randint(keys[4], (PASSAGES, DOC * DIM // 8), 0, 65536), jax.random.fold_in(keys[4], 1), 0, 65535).astype(jnp.int32)
    quantized_error_amounts = normal_values(keys[5], (4,), 0.05, 0.2, (), jnp.float32)
    keeper_document_position = draw_keeper_document_position(jax.random.fold_in(keys[8], 71), 0)
    active_keeper_tally = draw_active_keeper_tally(jax.random.fold_in(keys[8], 71), 0)
    return dict(request_term_embeds=request_term_embeds, cluster_means=cluster_means, cluster_shard_number=cluster_shard_number, cluster_entry_within=cluster_entry_within, quantized_error_words=quantized_error_words, quantized_error_amounts=quantized_error_amounts, keeper_document_position=keeper_document_position, active_keeper_tally=active_keeper_tally)


eps_norm = 1e-06
minimum_similarity = -1e+30

def unpack_residual(packed_words, quantized_error_amounts):
    shifts = 2 * jnp.arange(8, dtype=jnp.int32)
    codes = jnp.bitwise_and(jnp.right_shift(packed_words[..., None], shifts), 3)
    codes = codes.reshape(packed_words.shape[:-1] + (packed_words.shape[-1] * 8,))
    residual = jnp.zeros(codes.shape, jnp.float32)
    for level in range(4):
        residual = residual + jnp.where(codes == level, quantized_error_amounts[level].astype(jnp.float32), jnp.float32(0.0))
    return residual

def normalize_rows(values):
    values = values.astype(jnp.float32)
    return values * lax.rsqrt(lax.optimization_barrier(jnp.sum(values * values, axis=-1, keepdims=True)) + eps_norm)

def maxsim(request_embeds, document_embeds):
    similarity_matrix = jnp.einsum('td,nkd->tnk', request_embeds.astype(jnp.float32), document_embeds.astype(jnp.float32))
    return lax.optimization_barrier(jnp.sum(lax.optimization_barrier(jnp.max(similarity_matrix, axis=2)), axis=0))

def reference(request_term_embeds, cluster_means, cluster_shard_number, cluster_entry_within, quantized_error_words, quantized_error_amounts, keeper_document_position, active_keeper_tally):
    centroid_ids = cluster_shard_number[:, :, 0] * CENT_DEV + cluster_entry_within
    words = quantized_error_words.reshape(PASSAGES, DOC, DIM // 8)
    request_embed_lines = normalize_rows(request_term_embeds).astype(jnp.bfloat16)
    shard_first = jnp.arange(SHARD_TOTAL, dtype=jnp.int32)[:, None] * DOCS_PER_CHIP

    def lone_request(pair):
        request_embeds, local_ids = pair
        global_ids = (local_ids + shard_first).reshape(-1)
        rows_here = cluster_means[centroid_ids[global_ids]]
        residual = unpack_residual(words[global_ids], quantized_error_amounts)
        embedded = normalize_rows(rows_here.astype(jnp.float32) + residual).astype(jnp.bfloat16)
        cluster_similarity_matrix = maxsim(request_embeds, rows_here)
        exact_similarity_values = maxsim(request_embeds, embedded)
        return (cluster_similarity_matrix.reshape(SHARD_TOTAL, KEEPER_SEATS), exact_similarity_values.reshape(SHARD_TOTAL, KEEPER_SEATS))
    cluster_similarity_matrix, exact_similarity_values = lax.map(lone_request, (request_embed_lines, keeper_document_position))
    seat_active_flag = jnp.arange(KEEPER_SEATS, dtype=jnp.int32)[None, None, :] < active_keeper_tally[:, :, None]
    approx_scores = jnp.where(seat_active_flag, cluster_similarity_matrix, jnp.float32(0.0))
    exact_scores = jnp.where(seat_active_flag, exact_similarity_values, jnp.float32(0.0))
    flattened_similarities = jnp.where(seat_active_flag, exact_similarity_values, jnp.float32(minimum_similarity)).reshape(REQUEST_TOTAL, SHARD_TOTAL * KEEPER_SEATS)
    best_scores = lax.top_k(flattened_similarities, TOPK)[0]
    return (approx_scores, exact_scores, best_scores)
```

```python
import functools

import jax
import jax.numpy as jnp
from jax import lax
from jax.experimental import pallas as pl
from jax.experimental.pallas import tpu as pltpu
from jax.sharding import PartitionSpec as P

TOPK = 8
EPS = 1e-06
LOW = -1e30
MESH = pl.DeviceIdType.MESH
F32 = jnp.float32
BF16 = jnp.bfloat16
I32 = jnp.int32
VMEM = pltpu.VMEM
NT = (((1,), (1,)), ((), ()))


def iota(shape, axis):
    return lax.broadcasted_iota(I32, shape, axis)


def coords():
    x = lax.axis_index("query")
    z = lax.axis_index("corpus")
    yc = lax.axis_index("cent")
    return x, z, yc


def at_x(o, n, x):
    return {"query": lax.rem(x + o, n)}


def gather_kernel(X, Z, Y, means, qin, table, qall,
                  ysend, yrecv, qsend, qrecv, rsend, rrecv, lsend, lrecv, psend, precv, lsem):
    x, z, yc = coords()
    y, c = yc // 2, lax.rem(yc, 2)
    rows = table.shape[3]
    half = Z // 2
    up, down = {"corpus": lax.rem(z + 1, Z)}, {"corpus": lax.rem(z + Z - 1, Z)}
    mate = {"cent": y * 2 + 1 - c}

    mine = means.at[pl.ds(x * rows, rows)]
    own_t = pltpu.make_async_copy(mine, table.at[z, y, c], lsem.at[0])
    own_q = pltpu.make_async_copy(qin, qall.at[x], lsem.at[1])
    own_t.start()
    own_q.start()

    bar = pltpu.get_barrier_semaphore()
    peers = [up, down, mate]
    peers += [at_x(o, X, x) for o in range(1, X)]
    peers += [{"cent": lax.rem(y + o, Y) * 2 + c} for o in range(1, Y)]
    for d in peers:
        pl.semaphore_signal(bar, inc=1, device_id=d, device_id_type=MESH)
    pl.semaphore_wait(bar, len(peers))

    def copy(src, dst, s, r, d):
        return pltpu.make_async_remote_copy(
            src_ref=src, dst_ref=dst, send_sem=s, recv_sem=r, device_id=d, device_id_type=MESH)

    ycopies = []
    for o in range(1, Y):
        ycopies.append(copy(mine, table.at[z, y, c], ysend.at[o - 1], yrecv.at[o - 1],
                            {"cent": lax.rem(y + o, Y) * 2 + c}))
        ycopies[-1].start()
    qcopies = []
    for o in range(1, X):
        qcopies.append(copy(qin, qall.at[x], qsend.at[o - 1], qrecv.at[o - 1], at_x(o, X, x)))
        qcopies[-1].start()
    own_t.wait()
    for d in ycopies:
        d.wait_recv()

    hy = Y // 2

    def piece(zo, h):
        return table.at[zo, pl.ds(h * hy, hy), c]

    def to_mate(zo, h):
        copy(piece(zo, h), piece(zo, h), psend.at[0], precv.at[0], mate).start()

    def ring(s, h, right):
        zo = lax.rem(z + Z - s, Z) if right else lax.rem(z + s, Z)
        ss, rr = (rsend, rrecv) if right else (lsend, lrecv)
        return copy(piece(zo, h), piece(zo, h), ss.at[s, h], rr.at[s, h], up if right else down)

    sent = []

    def forward(s, h, right):
        if s + 1 < half or (s + 1 == half and h == (0 if right else 1)):
            d = ring(s, h, right)
            d.start()
            sent.append(d)

    for h in range(2):
        forward(0, h, True)
        forward(0, h, False)
    for h in range(2):
        to_mate(z, h)
    for s in range(1, half + 1):
        for h in range(2):
            for right in (True, False):
                if s == half and h != (0 if right else 1):
                    continue
                zo = lax.rem(z + Z - s, Z) if right else lax.rem(z + s, Z)
                ss, rr = (rsend, rrecv) if right else (lsend, lrecv)
                copy(piece(zo, h), piece(zo, h), ss.at[s - 1, h], rr.at[s - 1, h],
                     up if right else down).wait_recv()
                forward(s, h, right)
                to_mate(zo, h)
    own_q.wait()
    for d in qcopies:
        d.wait()
    for d in ycopies:
        d.wait_send()
    for d in sent:
        d.wait_send()
    whole = copy(table.at[:, :, c], table.at[:, :, 1 - c], psend.at[0], precv.at[0], mate)
    whole.wait_send()
    whole.wait_recv()


def gather_table(X, Z, Y, rows, means, queries):
    n = queries.shape[0]
    dma = pltpu.SemaphoreType.DMA
    half = Z // 2
    return pl.pallas_call(
        functools.partial(gather_kernel, X, Z, Y),
        out_shape=(jax.ShapeDtypeStruct((Z, Y, 2, rows, 128), BF16),
                   jax.ShapeDtypeStruct((X, n, 128), BF16)),
        in_specs=[pl.BlockSpec(memory_space=pl.ANY)] * 2,
        out_specs=(pl.BlockSpec(memory_space=VMEM),) * 2,
        scratch_shapes=[dma((Y - 1,)), dma((Y - 1,)), dma((X - 1,)), dma((X - 1,)),
                        dma((half, 2)), dma((half, 2)), dma((half, 2)), dma((half, 2)),
                        dma((1,)), dma((1,)), dma((2,))],
        compiler_params=pltpu.CompilerParams(
            collective_id=0, has_side_effects=True, vmem_limit_bytes=40 << 20),
        name="gather_table",
    )(means, queries)


def lookup_kernel(X, PP, idx, table, part, wide, got):
    total = table.shape[0]
    step = 512

    def widen(i, carry):
        r = pl.multiple_of(i * step, step)
        wide[pl.ds(r, step), :] = table[pl.ds(r, step), :].astype(F32)
        return carry

    lax.fori_loop(0, total // step, widen, 0)
    wide[pl.ds(total, 8), :] = jnp.zeros((8, 128), F32)

    def pick(i, carry):
        xx, tg = i // 64, lax.rem(i, 64)
        k = lax.rem(tg, 8) * 8 + tg // 8
        at = [idx[xx * PP + j, k] for j in range(PP)]
        rows = [wide[pl.ds(a, 1), :] for a in at]
        base = pl.multiple_of(i * PP, PP)
        for j in range(PP):
            got[pl.ds(base + j, 1), :] = rows[j]
        return carry

    lax.fori_loop(0, X * 64, pick, 0)
    part[...] = got[...].astype(BF16).reshape(part.shape)


def lookup(X, idx, table):
    PP = 64 // X
    total = table.shape[0]
    return pl.pallas_call(
        functools.partial(lookup_kernel, X, PP),
        out_shape=jax.ShapeDtypeStruct((X, 64 * PP, 128), BF16),
        in_specs=[pl.BlockSpec(memory_space=pltpu.SMEM), pl.BlockSpec(memory_space=VMEM)],
        out_specs=pl.BlockSpec(memory_space=VMEM),
        scratch_shapes=[VMEM((total + 8, 128), F32), VMEM((4096, 128), F32)],
        compiler_params=pltpu.CompilerParams(vmem_limit_bytes=40 << 20),
        name="lookup",
    )(idx, table)


def top8(v, base):
    lane = iota(v.shape, 1)
    cum = jnp.zeros((v.shape[0], 1), F32) + base.astype(F32) if not isinstance(base, int) else (
        jnp.full((v.shape[0], 1), float(base), F32))
    first = cum
    lanef = lane.astype(F32)
    out = jnp.zeros(v.shape, F32)
    for _ in range(TOPK):
        m = jnp.max(v, axis=1, keepdims=True)
        eq = v == m
        out = jnp.where(lanef >= cum, m, out)
        cum = cum + jnp.sum(jnp.where(eq, 1.0, 0.0), axis=1, keepdims=True)
        v = jnp.where(eq, -3e38, v)
    return jnp.where((lanef >= first) & (lanef < first + TOPK), out, 0.0)


def score_kernel(X, Z, YC, part, words, amounts, qall, pos, tally, approx, exact, best,
                 rbuf, wbuf, qn, res, dc, df, mp, st, sbuf, c1, c1buf, c2, c2buf,
                 wsem, xsend, xrecv, ssend, srecv, asend, arecv, bsend, brecv):
    x, z, yc = coords()
    PP = 64 // X
    NT_ROWS = 64 * PP
    wcopy = pltpu.make_async_copy(words.at[pl.ds(x * PP, PP)], wbuf, wsem.at[0])
    wcopy.start()

    xpeer = [at_x(o, X, x) for o in range(1, X)]
    cpeer = [{"cent": lax.rem(yc + o, YC)} for o in range(1, YC)]
    zpeer = [{"corpus": lax.rem(z + o, Z)} for o in range(1, Z)]
    bar = pltpu.get_barrier_semaphore()
    for d in zpeer + cpeer + xpeer:
        pl.semaphore_signal(bar, inc=1, device_id=d, device_id_type=MESH)
    pl.semaphore_wait(bar, X + YC + Z - 3)

    def copy(src, dst, s, r, d):
        return pltpu.make_async_remote_copy(
            src_ref=src, dst_ref=dst, send_sem=s, recv_sem=r, device_id=d, device_id_type=MESH)

    xcopies = []
    for o in range(1, X):
        xcopies.append(copy(part.at[lax.rem(x + o, X)], rbuf.at[o - 1],
                            xsend.at[o - 1], xrecv.at[o - 1], xpeer[o - 1]))
        xcopies[-1].start()

    q = qall[...].astype(F32)
    qn[...] = (q * lax.rsqrt(jnp.sum(q * q, axis=1, keepdims=True) + EPS)).astype(BF16)

    wcopy.wait()
    w = jnp.concatenate([wbuf[:, 128 * g:128 * (g + 1)] for g in range(8)], axis=0)
    lo = jnp.bitwise_and(w, 255).astype(F32).astype(BF16)
    hi = jnp.bitwise_and(jnp.right_shift(w, 8), 255).astype(F32).astype(BF16)
    bytes_ = jnp.concatenate([lo, hi], axis=1)
    col = iota((256, 1024), 1)
    d = jnp.bitwise_and(col, 127)
    want = (col // 128) * 16 + d // 8 + jnp.where(jnp.bitwise_and(d, 4) != 0, 128, 0)
    spread = jnp.where(iota((256, 1024), 0) == want, 1.0, 0.0).astype(BF16)
    got = jnp.dot(bytes_, spread, preferred_element_type=F32).astype(I32)
    lane = iota(got.shape, 1)
    low_bit = jnp.left_shift(1, 2 * jnp.bitwise_and(lane, 3))
    b0 = jnp.bitwise_and(got, low_bit) != 0
    b1 = jnp.bitwise_and(got, 2 * low_bit) != 0
    r = jnp.where(b1, jnp.where(b0, amounts[3], amounts[2]), jnp.where(b0, amounts[1], amounts[0]))
    for t in range(8):
        res[pl.ds(t * 8 * PP, 8 * PP), :] = r[:, 128 * t:128 * (t + 1)]

    spos = pos[...].astype(F32).astype(BF16)
    rep = jnp.where(jnp.bitwise_and(iota((16, 128), 1), 15) == iota((16, 128), 0), 1.0, 0.0)
    pos_t = jnp.dot(spos, rep.astype(BF16), preferred_element_type=F32).astype(I32)
    mp[...] = jnp.zeros_like(mp)

    for cp in xcopies:
        cp.wait()

    rows = part[x].astype(F32)
    for o in range(X - 1):
        rows = rows + rbuf[o].astype(F32)
    dc[...] = rows.astype(BF16)
    e = rows + res[...]
    df[...] = (e * lax.rsqrt(jnp.sum(e * e, axis=1, keepdims=True) + EPS)).astype(BF16)

    nq = qn.shape[0]
    blk = 256
    for which, docs in ((0, dc), (1, df)):
        row = pl.multiple_of(which * 64 + x * PP, PP)
        for n in range(nq // blk):
            sim = lax.dot_general(docs[...], qn[n * blk:(n + 1) * blk, :], NT,
                                  preferred_element_type=F32)
            mp[pl.ds(row, PP), n * blk:(n + 1) * blk] = jnp.max(sim.reshape(64, PP, blk), axis=0)
    ones = jnp.where(iota((nq // 32, nq), 1) // 32 == iota((nq // 32, nq), 0), 1.0, 0.0)
    st[...] = lax.dot_general(ones, mp[...], NT, precision=lax.Precision.HIGHEST,
                              preferred_element_type=F32)

    scopies = []
    for o in range(1, X):
        dst = pl.multiple_of(lax.rem(x + o, X) * 16, 16)
        scopies.append(copy(st.at[pl.ds(dst, 16)], sbuf.at[o - 1], ssend.at[o - 1],
                            srecv.at[o - 1], xpeer[o - 1]))
        scopies[-1].start()
    for cp in scopies:
        cp.wait()
    tot = st[pl.ds(pl.multiple_of(x * 16, 16), 16), :]
    for o in range(X - 1):
        tot = tot + sbuf[o]

    lane = iota((16, 128), 1)
    slot = jnp.bitwise_and(lane, 15)
    live = slot < tally[...]
    coarse = jnp.take_along_axis(tot, pos_t, axis=1, mode="promise_in_bounds")
    fine = jnp.take_along_axis(tot, pos_t + 64, axis=1, mode="promise_in_bounds")
    c1[...] = jnp.where(lane // 16 == yc, jnp.where(live, fine, LOW), 0.0)
    acopies = []
    for o in range(1, YC):
        acopies.append(copy(c1, c1buf.at[o - 1], asend.at[o - 1], arecv.at[o - 1], cpeer[o - 1]))
        acopies[-1].start()
    approx[...] = jnp.where(live, coarse, 0.0)[:, :16]
    exact[...] = jnp.where(live, fine, 0.0)[:, :16]
    for cp in acopies:
        cp.wait()
    v = c1[...]
    for o in range(YC - 1):
        v = v + c1buf[o]
    if YC * 16 < 128:
        v = jnp.where(lane < YC * 16, v, -2e38)
    c2[...] = top8(v, z * TOPK)
    bcopies = []
    for o in range(1, Z):
        bcopies.append(copy(c2, c2buf.at[o - 1], bsend.at[o - 1], brecv.at[o - 1], zpeer[o - 1]))
        bcopies[-1].start()
    for cp in bcopies:
        cp.wait()
    v = c2[...]
    for o in range(Z - 1):
        v = v + c2buf[o]
    if Z * TOPK < 128:
        v = jnp.where(lane < Z * TOPK, v, -2e38)
    best[...] = top8(v, 0)[:, :TOPK]


def score(X, Z, YC, part, words, amounts, qall, pos, tally):
    PP = 64 // X
    R = 64 * PP
    nq = qall.shape[0]
    dma = pltpu.SemaphoreType.DMA
    vm = pl.BlockSpec(memory_space=VMEM)
    f = functools.partial(jax.ShapeDtypeStruct, dtype=F32)
    return pl.pallas_call(
        functools.partial(score_kernel, X, Z, YC),
        out_shape=(f((16, 16)), f((16, 16)), f((16, TOPK))),
        in_specs=[vm, pl.BlockSpec(memory_space=pl.ANY), pl.BlockSpec(memory_space=pltpu.SMEM),
                  vm, vm, vm],
        out_specs=(vm, vm, vm),
        scratch_shapes=[
            VMEM((X - 1, R, 128), BF16), VMEM((PP, 1024), I32), VMEM((nq, 128), BF16),
            VMEM((R, 128), F32), VMEM((R, 128), BF16), VMEM((R, 128), BF16),
            VMEM((128, nq), F32), VMEM((nq // 32, 128), F32), VMEM((X - 1, 16, 128), F32),
            VMEM((16, 128), F32), VMEM((YC - 1, 16, 128), F32),
            VMEM((16, 128), F32), VMEM((Z - 1, 16, 128), F32),
            dma((1,)), dma((X - 1,)), dma((X - 1,)), dma((X - 1,)), dma((X - 1,)),
            dma((YC - 1,)), dma((YC - 1,)), dma((Z - 1,)), dma((Z - 1,)),
        ],
        compiler_params=pltpu.CompilerParams(
            collective_id=1, has_side_effects=True, vmem_limit_bytes=40 << 20),
        name="score",
    )(part, words, amounts, qall, pos, tally)


def local(request_term_embeds, cluster_means, cluster_shard_number, cluster_entry_within,
          quantized_error_words, quantized_error_amounts, keeper_document_position,
          active_keeper_tally):
    X, Z, YC = (lax.axis_size(a) for a in ("query", "corpus", "cent"))
    Y = YC // 2
    rows = cluster_means.shape[0] // X
    x = lax.axis_index("query")
    queries = request_term_embeds.reshape(-1, 128)
    table, qall = gather_table(X, Z, Y, rows, cluster_means, queries)
    shard = cluster_shard_number[:, :, 0]
    entry = cluster_entry_within
    idx = jnp.where(entry // rows == x, shard * rows + entry % rows, Z * YC * rows)
    part = lookup(X, idx, table.reshape(-1, 128))
    approx, exact, best = score(
        X, Z, YC, part, quantized_error_words, quantized_error_amounts,
        qall.reshape(-1, 128), keeper_document_position[:, 0, :], active_keeper_tally)
    return approx[:, None, :], exact[:, None, :], best


def solution(mesh):
    return jax.shard_map(
        local,
        mesh=mesh,
        in_specs=(
            P("query", None, None),
            P(("corpus", "cent"), None),
            P(("corpus", "cent"), None, None),
            P(("corpus", "cent"), None),
            P(("corpus", "cent"), None),
            P(),
            P("query", ("corpus", "cent"), None),
            P("query", ("corpus", "cent")),
        ),
        out_specs=(
            P("query", ("corpus", "cent"), None),
            P("query", ("corpus", "cent"), None),
            P("query", None),
        ),
        check_vma=False,
    )
```

```python
import collections
import functools

import jax
import jax.numpy as jnp
from jax import lax
from jax.experimental import pallas as pl
from jax.experimental.pallas import tpu as pltpu
from jax.sharding import PartitionSpec as P

TOPK = 8
EPS = 1e-06
LOW = -1e30
MESH = pl.DeviceIdType.MESH
F32 = jnp.float32
BF16 = jnp.bfloat16
I32 = jnp.int32
VMEM = pltpu.VMEM
NT = (((1,), (1,)), ((), ()))
CHUNKS = 4


def iota(shape, axis):
    return lax.broadcasted_iota(I32, shape, axis)


def remote(src, dst, s, r, d):
    return pltpu.make_async_remote_copy(
        src_ref=src, dst_ref=dst, send_sem=s, recv_sem=r, device_id=d, device_id_type=MESH)


def top8(v, base):
    lane = iota(v.shape, 1).astype(F32)
    first = jnp.zeros((v.shape[0], 1), F32) + jnp.asarray(base).astype(F32)
    cum = first
    out = jnp.zeros(v.shape, F32)
    for _ in range(TOPK):
        m = jnp.max(v, axis=1, keepdims=True)
        eq = v == m
        out = jnp.where(lane >= cum, m, out)
        cum = cum + jnp.sum(jnp.where(eq, 1.0, 0.0), axis=1, keepdims=True)
        v = jnp.where(eq, -3e38, v)
    return jnp.where((lane >= first) & (lane < first + TOPK), out, 0.0)


def kernel(X, Z, Y, means, qin, shard, entry, words, amounts, pos, tally, out,
           table, wide, qall, qn, shard_v, entry_v, idx_v, idx, wbuf, spread, res, got, own,
           part, rbuf, dc, df, mp, st, sbuf, c1, c1buf, c2, c2buf,
           lsem, rsend, rrecv, lsend, lrecv, ysend, yrecv, qsend, qrecv, psend, precv,
           xsend, xrecv, ssend, srecv, asend, arecv, bsend, brecv):
    x = lax.axis_index("query")
    z = lax.axis_index("corpus")
    yc = lax.axis_index("cent")
    YC = 2 * Y
    y, c = yc // 2, lax.rem(yc, 2)
    PP = 64 // X
    rows = table.shape[3]
    hr = rows // 2
    half = Z // 2
    total = Z * YC * rows
    R = 64 * PP
    CR = R // CHUNKS

    mine = means.at[pl.ds(x * rows, rows)]
    locals_ = [
        pltpu.make_async_copy(mine, table.at[z, y, c], lsem.at[0]),
        pltpu.make_async_copy(qin, qall.at[x], lsem.at[1]),
        pltpu.make_async_copy(shard, shard_v, lsem.at[2]),
        pltpu.make_async_copy(entry, entry_v, lsem.at[3]),
        pltpu.make_async_copy(words.at[pl.ds(x * PP, PP)], wbuf, lsem.at[4]),
    ]
    for d in locals_:
        d.start()

    up, down = {"corpus": lax.rem(z + 1, Z)}, {"corpus": lax.rem(z + Z - 1, Z)}
    mate = {"cent": y * 2 + 1 - c}
    ypeer = [{"cent": lax.rem(y + o, Y) * 2 + c} for o in range(1, Y)]
    xpeer = [{"query": lax.rem(x + o, X)} for o in range(1, X)]
    cpeer = [{"cent": lax.rem(yc + o, YC)} for o in range(1, YC)]
    zpeer = [{"corpus": lax.rem(z + o, Z)} for o in range(1, Z)]
    bar = pltpu.get_barrier_semaphore()
    near = [up, down, mate] + ypeer + xpeer
    for d in near:
        pl.semaphore_signal(bar, inc=1, device_id=d, device_id_type=MESH)
    pl.semaphore_wait(bar, len(near))

    def origin(s, right):
        return lax.rem(z + Z - s, Z) if right else lax.rem(z + s, Z)

    def ref(zo, yo, h):
        return table.at[zo, yo, c, pl.ds(h * hr, hr)]

    def last(h, right):
        return half if (h == 0) == right else half - 1

    def ring(h, s, right):
        r = ref(origin(s, right), y, h)
        return remote(r, r, (rsend if right else lsend).at[h, s], (rrecv if right else lrecv).at[h, s],
                      up if right else down)

    def slot(s, right):
        return s if right else half + s

    def ycopy(h, s, right, o, back):
        yo = lax.rem(y + Y - o, Y) if back else y
        r = ref(origin(s, right), yo, h)
        return remote(r, r, ysend.at[o - 1], yrecv.at[h, slot(s, right), o - 1], ypeer[o - 1])

    def widen(zo, yo, h, cc, n):
        base = pl.multiple_of(((zo * Y + yo) * 2 + cc) * rows + h * hr, hr)
        wide[pl.ds(base, n), :] = table[zo, yo, cc, pl.ds(h * hr, n), :].astype(F32)

    def to_mate(zo, yo, h):
        r = ref(zo, yo, h)
        remote(r, r, psend.at[0], precv.at[0], mate).start()

    sent = []
    pending = collections.deque()

    def forward(h, s, right):
        if s < last(h, right):
            d = ring(h, s, right)
            d.start()
            sent.append(d)

    def spread_out(h, s, right):
        for o in range(1, Y):
            ycopy(h, s, right, o, False).start()
        pending.append((h, s, right))
        to_mate(origin(s, right), y, h)

    def collect(upto):
        while pending and pending[0][1] <= upto:
            h, s, right = pending.popleft()
            for o in range(1, Y):
                ycopy(h, s, right, o, True).wait_recv()
                yo = lax.rem(y + Y - o, Y)
                to_mate(origin(s, right), yo, h)
                widen(origin(s, right), yo, h, c, hr)

    def make_index():
        locals_[2].wait()
        locals_[3].wait()
        e = entry_v[...]
        idx_v[...] = jnp.where(e // rows == x, shard_v[...] * rows + lax.rem(e, rows), total)
        for o in range(X):
            src = idx_v.at[pl.ds(pl.multiple_of(lax.rem(x + o, X) * PP, PP), PP)]
            pltpu.make_async_copy(src, idx.at[pl.ds(o * PP, PP)], lsem.at[5 + o]).start()
        wide[pl.ds(total, 8), :] = jnp.zeros((8, 128), F32)

    def make_spread():
        col = iota((256, 1024), 1)
        d = jnp.bitwise_and(col, 127)
        want = (col // 128) * 16 + d // 8 + jnp.where(jnp.bitwise_and(d, 4) != 0, 128, 0)
        spread[...] = jnp.where(iota((256, 1024), 0) == want, 1.0, 0.0).astype(BF16)

    def decode():
        locals_[4].wait()
        w = jnp.concatenate([wbuf[:, 128 * g:128 * (g + 1)] for g in range(8)], axis=0)
        lo = jnp.bitwise_and(w, 255).astype(F32).astype(BF16)
        hi = jnp.bitwise_and(jnp.right_shift(w, 8), 255).astype(F32).astype(BF16)
        code = jnp.dot(jnp.concatenate([lo, hi], axis=1), spread[...],
                       preferred_element_type=F32).astype(I32)
        bit = jnp.left_shift(1, 2 * jnp.bitwise_and(iota(code.shape, 1), 3))
        b0 = jnp.bitwise_and(code, bit) != 0
        b1 = jnp.bitwise_and(code, 2 * bit) != 0
        r = jnp.where(b1, jnp.where(b0, amounts[3], amounts[2]), jnp.where(b0, amounts[1], amounts[0]))
        for t in range(8):
            res[pl.ds(t * 8 * PP, 8 * PP), :] = r[:, 128 * t:128 * (t + 1)]

    def normalize(k):
        q = qall[k].astype(F32)
        n = q.shape[0]
        qn[pl.ds(pl.multiple_of(k * n, n), n), :] = (
            q * lax.rsqrt(jnp.sum(q * q, axis=1, keepdims=True) + EPS)).astype(BF16)

    def normalize_own():
        locals_[1].wait()
        normalize(x)

    def normalize_peer(o):
        remote(qin, qall.at[x], qsend.at[o - 1], qrecv.at[o - 1], xpeer[o - 1]).wait()
        normalize(lax.rem(x + X - o, X))

    work = collections.deque([make_index, make_spread, decode, normalize_own] +
                             [functools.partial(normalize_peer, o) for o in range(1, X)])

    locals_[0].wait()
    for h in range(2):
        forward(h, 0, True)
        forward(h, 0, False)
    for o in range(1, X):
        remote(qin, qall.at[x], qsend.at[o - 1], qrecv.at[o - 1], xpeer[o - 1]).start()
    for h in range(2):
        spread_out(h, 0, True)
    widen(z, y, 0, c, rows)
    work.popleft()()
    for s in range(1, half + 1):
        for h in range(2):
            for right in (True, False):
                if s <= last(h, right):
                    r = ref(origin(s, right), y, h)
                    remote(r, r, (rsend if right else lsend).at[h, s - 1],
                           (rrecv if right else lrecv).at[h, s - 1], up if right else down).wait_recv()
                    forward(h, s, right)
                    spread_out(h, s, right)
                    widen(origin(s, right), y, h, c, hr)
        if work:
            work.popleft()()
        collect(s - 2)
    while work:
        work.popleft()()
    collect(half)
    whole = remote(table.at[:, :, c], table.at[:, :, 1 - c], psend.at[0], precv.at[0], mate)
    whole.wait_recv()

    def widen_mate(i, carry):
        for yo in range(Y):
            widen(i, yo, 0, 1 - c, rows)
        return carry

    lax.fori_loop(0, Z, widen_mate, 0)
    for o in range(X):
        pltpu.make_async_copy(idx_v.at[pl.ds(0, PP)], idx.at[pl.ds(o * PP, PP)], lsem.at[5 + o]).wait()

    tc = 8 // CHUNKS

    def xcopy(o, ch):
        piece = pl.ds(ch * CR, CR)
        return remote(part.at[o - 1, piece], rbuf.at[o - 1, piece], xsend.at[o - 1, ch],
                      xrecv.at[o - 1, ch], xpeer[o - 1])

    order = [o for o in (2, 1, 3) if o < X] + [o for o in range(4, X)]
    for ch in range(CHUNKS):
        for o in order + [0]:
            def pick(g, carry, o=o, ch=ch):
                for t in range(tc):
                    k = 8 * g + ch * tc + t
                    picked = [wide[pl.ds(idx[o * PP + j, k], 1), :] for j in range(PP)]
                    base = pl.multiple_of(g * PP + t * 8 * PP, PP)
                    for j in range(PP):
                        if o:
                            got[pl.ds(base + j, 1), :] = picked[j]
                        else:
                            own[pl.ds(base + ch * CR + j, 1), :] = picked[j]
                return carry

            lax.fori_loop(0, 8, pick, 0)
            if o:
                part[o - 1, ch * CR:(ch + 1) * CR, :] = got[...].astype(BF16)
                xcopy(o, ch).start()

    mp[...] = jnp.zeros_like(mp)
    nq = qn.shape[0]
    blk = 256
    for ch in range(CHUNKS):
        a, b = ch * CR, (ch + 1) * CR
        v = own[a:b, :]
        for o in order:
            xcopy(o, ch).wait()
            v = v + rbuf[o - 1, a:b, :].astype(F32)
        dc[...] = v.astype(BF16)
        e = v + res[a:b, :]
        df[...] = (e * lax.rsqrt(jnp.sum(e * e, axis=1, keepdims=True) + EPS)).astype(BF16)
        for which, docs in ((0, dc), (1, df)):
            row = pl.multiple_of(which * 64 + x * PP, PP)
            for n in range(nq // blk):
                sim = lax.dot_general(docs[...], qn[n * blk:(n + 1) * blk, :], NT,
                                      preferred_element_type=F32)
                m = jnp.max(sim.reshape(CR // PP, PP, blk), axis=0)
                if ch:
                    m = jnp.maximum(m, mp[pl.ds(row, PP), n * blk:(n + 1) * blk])
                mp[pl.ds(row, PP), n * blk:(n + 1) * blk] = m
    ones = jnp.where(iota((nq // 32, nq), 1) // 32 == iota((nq // 32, nq), 0), 1.0, 0.0)
    st[...] = lax.dot_general(ones, mp[...], NT, precision=lax.Precision.HIGHEST,
                              preferred_element_type=F32)

    scopies = []
    for o in range(1, X):
        dst = pl.multiple_of(lax.rem(x + o, X) * 16, 16)
        scopies.append(remote(st.at[pl.ds(dst, 16)], sbuf.at[o - 1], ssend.at[o - 1],
                              srecv.at[o - 1], xpeer[o - 1]))
        scopies[-1].start()

    lane = iota((16, 128), 1)
    rep = jnp.where(jnp.bitwise_and(lane, 15) == iota((16, 128), 0), 1.0, 0.0).astype(BF16)
    pos_t = jnp.dot(pos[...].astype(F32).astype(BF16), rep, preferred_element_type=F32).astype(I32)
    count = jnp.sum(jnp.where(iota((16, 16), 0) == iota((16, 16), 1), tally[...], 0),
                    axis=1, keepdims=True)
    live = jnp.bitwise_and(lane, 15) < count
    for cp in scopies:
        cp.wait()
    tot = st[pl.ds(pl.multiple_of(x * 16, 16), 16), :]
    for o in range(X - 1):
        tot = tot + sbuf[o]
    fine = jnp.take_along_axis(tot, pos_t + 64, axis=1, mode="promise_in_bounds")
    c1[...] = jnp.where(lane // 16 == yc, jnp.where(live, fine, LOW), 0.0)
    acopies = []
    for o in range(1, YC):
        acopies.append(remote(c1, c1buf.at[o - 1], asend.at[o - 1], arecv.at[o - 1], cpeer[o - 1]))
        acopies[-1].start()
    coarse = jnp.take_along_axis(tot, pos_t, axis=1, mode="promise_in_bounds")
    scores = jnp.where(live, jnp.where(lane < 16, coarse, fine), 0.0)
    for cp in acopies:
        cp.wait()
    v = c1[...]
    for o in range(YC - 1):
        v = v + c1buf[o]
    c2[...] = top8(v, z * TOPK)
    bcopies = []
    for o in range(1, Z):
        bcopies.append(remote(c2, c2buf.at[o - 1], bsend.at[o - 1], brecv.at[o - 1], zpeer[o - 1]))
        bcopies[-1].start()
    for d in sent:
        d.wait_send()
    for o in range(1, Y):
        r = table.at[:, y, c]
        remote(r, r, ysend.at[o - 1], yrecv.at[0, 0, o - 1], ypeer[o - 1]).wait_send()
    whole.wait_send()
    for cp in bcopies:
        cp.wait()
    v = c2[...]
    for o in range(Z - 1):
        v = v + c2buf[o]
    out[...] = jnp.where(lane < 32, scores, top8(v, 32))


def fused(X, Z, YC, means, queries, shard, entry, words, amounts, pos, tally):
    PP = 64 // X
    R = 64 * PP
    CR = R // CHUNKS
    Y = YC // 2
    rows = means.shape[0] // X
    half = Z // 2
    n = queries.shape[0]
    nq = X * n
    dma = pltpu.SemaphoreType.DMA
    vm = pl.BlockSpec(memory_space=VMEM)
    hbm = pl.BlockSpec(memory_space=pltpu.HBM)
    return pl.pallas_call(
        functools.partial(kernel, X, Z, Y),
        out_shape=jax.ShapeDtypeStruct((16, 128), F32),
        in_specs=[hbm, hbm, hbm, hbm, hbm, pl.BlockSpec(memory_space=pltpu.SMEM), vm, vm],
        out_specs=vm,
        scratch_shapes=[
            VMEM((Z, Y, 2, rows, 128), BF16), VMEM((Z * YC * rows + 8, 128), F32),
            VMEM((X, n, 128), BF16), VMEM((nq, 128), BF16),
            VMEM((64, 64), I32), VMEM((64, 64), I32), VMEM((64, 64), I32),
            pltpu.SMEM((64, 64), I32), VMEM((PP, 1024), I32), VMEM((256, 1024), BF16),
            VMEM((R, 128), F32), VMEM((CR, 128), F32), VMEM((R, 128), F32),
            VMEM((X - 1, R, 128), BF16), VMEM((X - 1, R, 128), BF16),
            VMEM((CR, 128), BF16), VMEM((CR, 128), BF16),
            VMEM((128, nq), F32), VMEM((nq // 32, 128), F32), VMEM((X - 1, 16, 128), F32),
            VMEM((16, 128), F32), VMEM((YC - 1, 16, 128), F32),
            VMEM((16, 128), F32), VMEM((Z - 1, 16, 128), F32),
            dma((5 + X,)),
            dma((2, half)), dma((2, half)), dma((2, half)), dma((2, half)),
            dma((Y - 1,)), dma((2, 2 * half + 1, Y - 1)),
            dma((X - 1,)), dma((X - 1,)), dma((1,)), dma((1,)),
            dma((X - 1, CHUNKS)), dma((X - 1, CHUNKS)), dma((X - 1,)), dma((X - 1,)),
            dma((YC - 1,)), dma((YC - 1,)), dma((Z - 1,)), dma((Z - 1,)),
        ],
        compiler_params=pltpu.CompilerParams(
            collective_id=0, has_side_effects=True, vmem_limit_bytes=60 << 20),
        name="plaid",
    )(means, queries, shard, entry, words, amounts, pos, tally)


def local(request_term_embeds, cluster_means, cluster_shard_number, cluster_entry_within,
          quantized_error_words, quantized_error_amounts, keeper_document_position,
          active_keeper_tally):
    X, Z, YC = (lax.axis_size(a) for a in ("query", "corpus", "cent"))
    out = fused(X, Z, YC, cluster_means, request_term_embeds.reshape(-1, 128),
                cluster_shard_number[:, :, 0], cluster_entry_within, quantized_error_words,
                quantized_error_amounts, keeper_document_position[:, 0, :],
                active_keeper_tally.reshape(1, 16))
    return out[:, None, 0:16], out[:, None, 16:32], out[:, 32:32 + TOPK]


def solution(mesh):
    return jax.shard_map(
        local,
        mesh=mesh,
        in_specs=(
            P("query", None, None),
            P(("corpus", "cent"), None),
            P(("corpus", "cent"), None, None),
            P(("corpus", "cent"), None),
            P(("corpus", "cent"), None),
            P(),
            P("query", ("corpus", "cent"), None),
            P("query", ("corpus", "cent")),
        ),
        out_specs=(
            P("query", ("corpus", "cent"), None),
            P("query", ("corpus", "cent"), None),
            P("query", None),
        ),
        check_vma=False,
    )
```

```python
import collections
import functools

import jax
import jax.numpy as jnp
from jax import lax
from jax.experimental import pallas as pl
from jax.experimental.pallas import tpu as pltpu
from jax.sharding import PartitionSpec as P

TOPK = 8
EPS = 1e-06
LOW = -1e30
MESH = pl.DeviceIdType.MESH
F32 = jnp.float32
BF16 = jnp.bfloat16
I32 = jnp.int32
VMEM = pltpu.VMEM
NT = (((1,), (1,)), ((), ()))
CHUNKS = 4


def iota(shape, axis):
    return lax.broadcasted_iota(I32, shape, axis)


def remote(src, dst, s, r, d):
    return pltpu.make_async_remote_copy(
        src_ref=src, dst_ref=dst, send_sem=s, recv_sem=r, device_id=d, device_id_type=MESH)


def top8(vs, base):
    lane = iota(vs[0].shape, 1).astype(F32)
    first = jnp.zeros((vs[0].shape[0], 1), F32) + base
    cum = first
    out = jnp.zeros(vs[0].shape, F32)
    for _ in range(TOPK):
        m = jnp.max(functools.reduce(jnp.maximum, vs), axis=1, keepdims=True)
        out = jnp.where(lane >= cum, m, out)
        equal = [v == m for v in vs]
        seen = functools.reduce(jnp.add, [jnp.where(e, 1.0, 0.0) for e in equal])
        cum = cum + jnp.sum(seen, axis=1, keepdims=True)
        vs = [jnp.where(e, -3e38, v) for e, v in zip(equal, vs)]
    return jnp.where((lane >= first) & (lane < first + TOPK), out, 0.0)


def kernel(X, Z, Y, means, qin, shard, entry, words, amounts, pos, tally, out,
           table, wide, qall, qn, shard_v, entry_v, idx_v, idx, wbuf, spread, res, got, own,
           part, rbuf, dc, df, mp, st, sbuf, pos_all, tal_all, keep, c1, c1buf, c2, c2buf,
           lsem, rsend, rrecv, lsend, lrecv, ysend, yrecv, qsend, qrecv, psend, precv, tsend, trecv,
           xsend, xrecv, ssend, srecv, asend, arecv, bsend, brecv):
    x = lax.axis_index("query")
    z = lax.axis_index("corpus")
    yc = lax.axis_index("cent")
    YC = 2 * Y
    y, c = yc // 2, lax.rem(yc, 2)
    PP = 64 // X
    rows = table.shape[3]
    hr = rows // 2
    half = Z // 2
    total = Z * YC * rows
    R = 64 * PP
    CR = R // CHUNKS

    mine = means.at[pl.ds(x * rows, rows)]
    locals_ = [
        pltpu.make_async_copy(mine, table.at[z, y, c], lsem.at[0]),
        pltpu.make_async_copy(qin, qall.at[x], lsem.at[1]),
        pltpu.make_async_copy(shard, shard_v, lsem.at[2]),
        pltpu.make_async_copy(entry, entry_v, lsem.at[3]),
        pltpu.make_async_copy(words.at[pl.ds(x * PP, PP)], wbuf, lsem.at[4]),
    ]
    for d in locals_:
        d.start()

    zdev = {(k, r): {"corpus": lax.rem(z + (k if r else Z - k), Z)} for k in (1, 2) for r in (True, False)}
    mate = {"cent": y * 2 + 1 - c}
    ypeer = [{"cent": lax.rem(y + o, Y) * 2 + c} for o in range(1, Y)]
    xpeer = [{"query": lax.rem(x + o, X)} for o in range(1, X)]
    zpeer = [{"corpus": lax.rem(z + o, Z)} for o in range(1, Z)]
    bar = pltpu.get_barrier_semaphore()
    near = list(zdev.values()) + [mate] + ypeer + xpeer
    for d in near:
        pl.semaphore_signal(bar, inc=1, device_id=d, device_id_type=MESH)
    pl.semaphore_wait(bar, len(near))

    def origin(s, right):
        return lax.rem(z + Z - s, Z) if right else lax.rem(z + s, Z)

    def ref(zo, yo, h):
        return table.at[zo, yo, c, pl.ds(h * hr, hr)]

    def last(h, right):
        return half if (h == 0) == right else half - 1

    def ring(h, s, right, hop):
        r = ref(origin(s, right), y, h)
        return remote(r, r, (rsend if right else lsend).at[h, s + hop - 1],
                      (rrecv if right else lrecv).at[h, s + hop - 1], zdev[hop, right])

    def slot(s, right):
        return s if right else half + s

    def ycopy(h, s, right, yo, to, tag):
        r = ref(origin(s, right), yo, h)
        return remote(r, r, ysend.at[tag - 1], yrecv.at[h, slot(s, right), tag - 1], ypeer[to - 1])

    def widen(zo, yo, h, cc, n):
        base = pl.multiple_of(((zo * Y + yo) * 2 + cc) * rows + h * hr, hr)
        wide[pl.ds(base, n), :] = table[zo, yo, cc, pl.ds(h * hr, n), :].astype(F32)

    def to_mate(zo, yo, h):
        r = ref(zo, yo, h)
        remote(r, r, psend.at[0], precv.at[0], mate).start()

    sent = []
    pending, relayed = collections.deque(), collections.deque()

    def forward(h, s, right, hop):
        if s + hop <= last(h, right):
            d = ring(h, s, right, hop)
            d.start()
            sent.append(d)

    def along_y(h, s, right):
        for o in (1, Y - 1):
            ycopy(h, s, right, y, o, o).start()
        pending.append((h, s, right))

    def collect(upto):
        while pending and pending[0][1] <= upto:
            h, s, right = pending.popleft()
            for o in (1, Y - 1):
                ycopy(h, s, right, lax.rem(y + Y - o, Y), o, o).wait_recv()
                if (h == 0) == (o == 1):
                    ycopy(h, s, right, lax.rem(y + Y - o, Y), o, 2).start()
            for o in (1, Y - 1):
                to_mate(origin(s, right), lax.rem(y + Y - o, Y), h)
            for o in (1, Y - 1):
                widen(origin(s, right), lax.rem(y + Y - o, Y), h, c, hr)
            relayed.append((h, s, right))

    def collect_relayed(upto):
        while relayed and relayed[0][1] <= upto:
            h, s, right = relayed.popleft()
            yo = lax.rem(y + 2, Y)
            ycopy(h, s, right, yo, 1, 2).wait_recv()
            to_mate(origin(s, right), yo, h)
            widen(origin(s, right), yo, h, c, hr)

    def make_index():
        locals_[2].wait()
        locals_[3].wait()
        e = entry_v[...]
        idx_v[...] = jnp.where(e // rows == x, shard_v[...] * rows + lax.rem(e, rows), total)
        for o in range(X):
            src = idx_v.at[pl.ds(pl.multiple_of(lax.rem(x + o, X) * PP, PP), PP)]
            pltpu.make_async_copy(src, idx.at[pl.ds(o * PP, PP)], lsem.at[5 + o]).start()
        wide[pl.ds(total, 8), :] = jnp.zeros((8, 128), F32)

    def make_spread():
        col = iota((256, 1024), 1)
        d = jnp.bitwise_and(col, 127)
        want = (col // 128) * 16 + d // 8 + jnp.where(jnp.bitwise_and(d, 4) != 0, 128, 0)
        spread[...] = jnp.where(iota((256, 1024), 0) == want, 1.0, 0.0).astype(BF16)

    def decode():
        locals_[4].wait()
        w = jnp.concatenate([wbuf[:, 128 * g:128 * (g + 1)] for g in range(8)], axis=0)
        lo = jnp.bitwise_and(w, 255).astype(F32).astype(BF16)
        hi = jnp.bitwise_and(jnp.right_shift(w, 8), 255).astype(F32).astype(BF16)
        code = jnp.dot(jnp.concatenate([lo, hi], axis=1), spread[...],
                       preferred_element_type=F32).astype(I32)
        bit = jnp.left_shift(1, 2 * jnp.bitwise_and(iota(code.shape, 1), 3))
        b0 = jnp.bitwise_and(code, bit) != 0
        b1 = jnp.bitwise_and(code, 2 * bit) != 0
        r = jnp.where(b1, jnp.where(b0, amounts[3], amounts[2]), jnp.where(b0, amounts[1], amounts[0]))
        for t in range(8):
            res[pl.ds(t * 8 * PP, 8 * PP), :] = r[:, 128 * t:128 * (t + 1)]

    def normalize(k):
        q = qall[k].astype(F32)
        n = q.shape[0]
        qn[pl.ds(pl.multiple_of(k * n, n), n), :] = (
            q * lax.rsqrt(jnp.sum(q * q, axis=1, keepdims=True) + EPS)).astype(BF16)

    def normalize_own():
        locals_[1].wait()
        normalize(x)

    def normalize_peer(o):
        remote(qin, qall.at[x], qsend.at[o - 1], qrecv.at[o - 1], xpeer[o - 1]).wait()
        normalize(lax.rem(x + X - o, X))

    lane = iota((16, 128), 1)
    fine0 = 64 * c + PP * x
    coarse0 = 64 * (1 - c) + PP * x

    def keep_rows(k):
        p = pos_all[k]
        count = jnp.sum(jnp.where(iota((16, 16), 0) == iota((16, 16), 1), tal_all[k], 0),
                        axis=1, keepdims=True)
        p = jnp.where(iota((16, 16), 1) < count, p, -1000)
        kept = jnp.zeros((16, 128), I32)
        for j in range(16):
            kept = jnp.where(p[:, j:j + 1] - PP * x == lane - fine0, 1, kept)
        kept = jnp.where((lane >= fine0) & (lane < fine0 + PP), kept, 2)
        keep[pl.ds(pl.multiple_of(k * 16, 16), 16), :] = kept

    def keep_peer(o):
        remote(pos, pos_all.at[x], tsend.at[0, o - 1], trecv.at[0, o - 1], xpeer[o - 1]).wait()
        remote(tally, tal_all.at[x], tsend.at[1, o - 1], trecv.at[1, o - 1], xpeer[o - 1]).wait()
        keep_rows(lax.rem(x + X - o, X))

    def keep_own():
        pos_all[x] = pos[...]
        tal_all[x] = tally[...]
        keep_rows(x)

    def keep_all():
        keep_own()
        for o in range(1, X):
            keep_peer(o)

    work = collections.deque([make_index, make_spread, keep_all, decode, normalize_own] +
                             [functools.partial(normalize_peer, o) for o in range(1, X)])

    locals_[0].wait()
    for hop in (1, 2):
        for h in range(2):
            forward(h, 0, True, hop)
            forward(h, 0, False, hop)
    for h in range(2):
        along_y(h, 0, True)
    for o in range(1, X):
        remote(pos, pos_all.at[x], tsend.at[0, o - 1], trecv.at[0, o - 1], xpeer[o - 1]).start()
        remote(tally, tal_all.at[x], tsend.at[1, o - 1], trecv.at[1, o - 1], xpeer[o - 1]).start()
        remote(qin, qall.at[x], qsend.at[o - 1], qrecv.at[o - 1], xpeer[o - 1]).start()
    for h in range(2):
        to_mate(z, y, h)
    widen(z, y, 0, c, rows)
    work.popleft()()
    for s in range(1, half + 1):
        here = [(h, right) for h in range(2) for right in (True, False) if s <= last(h, right)]
        for h, right in here:
            r = ref(origin(s, right), y, h)
            remote(r, r, (rsend if right else lsend).at[h, s - 1],
                   (rrecv if right else lrecv).at[h, s - 1], zdev[1, right]).wait_recv()
            forward(h, s, right, 2)
        for h, right in here:
            along_y(h, s, right)
        for h, right in here:
            to_mate(origin(s, right), y, h)
        for h, right in here:
            widen(origin(s, right), y, h, c, hr)
        collect(s - 2)
        collect_relayed(s - 4)
        if work:
            work.popleft()()
    while work:
        work.popleft()()
    collect(half)
    collect_relayed(half)
    whole = remote(table.at[:, :, c], table.at[:, :, 1 - c], psend.at[0], precv.at[0], mate)
    whole.wait_recv()

    def widen_mate(i, carry):
        for yo in range(Y):
            widen(i, yo, 0, 1 - c, rows)
        return carry

    lax.fori_loop(0, Z, widen_mate, 0)
    for o in range(X):
        pltpu.make_async_copy(idx_v.at[pl.ds(0, PP)], idx.at[pl.ds(o * PP, PP)], lsem.at[5 + o]).wait()

    tc = 8 // CHUNKS

    def xcopy(o, ch):
        piece = pl.ds(ch * CR, CR)
        return remote(part.at[o - 1, piece], rbuf.at[o - 1, piece], xsend.at[o - 1, ch],
                      xrecv.at[o - 1, ch], xpeer[o - 1])

    order = [o for o in (2, 1, 3) if o < X] + [o for o in range(4, X)]
    for ch in range(CHUNKS):
        for o in order + [0]:
            def pick(g, carry, o=o, ch=ch):
                for t in range(tc):
                    k = 8 * g + ch * tc + t
                    picked = [wide[pl.ds(idx[o * PP + j, k], 1), :] for j in range(PP)]
                    base = pl.multiple_of(g * PP + t * 8 * PP, PP)
                    for j in range(PP):
                        if o:
                            got[pl.ds(base + j, 1), :] = picked[j]
                        else:
                            own[pl.ds(base + ch * CR + j, 1), :] = picked[j]
                return carry

            lax.fori_loop(0, 8, pick, 0)
            if o:
                part[o - 1, ch * CR:(ch + 1) * CR, :] = got[...].astype(BF16)
                xcopy(o, ch).start()

    mp[...] = jnp.zeros_like(mp)
    nq = qn.shape[0]
    blk = 256
    for ch in range(CHUNKS):
        a, b = ch * CR, (ch + 1) * CR
        v = own[a:b, :]
        for o in order:
            xcopy(o, ch).wait()
            v = v + rbuf[o - 1, a:b, :].astype(F32)
        dc[...] = v.astype(BF16)
        e = v + res[a:b, :]
        df[...] = (e * lax.rsqrt(jnp.sum(e * e, axis=1, keepdims=True) + EPS)).astype(BF16)
        for which, docs in ((0, dc), (1, df)):
            row = pl.multiple_of(fine0 if which else coarse0, PP)
            for n in range(nq // blk):
                sim = lax.dot_general(docs[...], qn[n * blk:(n + 1) * blk, :], NT,
                                      preferred_element_type=F32)
                m = jnp.max(sim.reshape(CR // PP, PP, blk), axis=0)
                if ch:
                    m = jnp.maximum(m, mp[pl.ds(row, PP), n * blk:(n + 1) * blk])
                mp[pl.ds(row, PP), n * blk:(n + 1) * blk] = m
    ones = jnp.where(iota((nq // 32, nq), 1) // 32 == iota((nq // 32, nq), 0), 1.0, 0.0)
    st[...] = lax.dot_general(ones, mp[...], NT, precision=lax.Precision.HIGHEST,
                              preferred_element_type=F32)

    wide_lane, wide_row = iota(st.shape, 1), iota(st.shape, 0)
    v = jnp.where(keep[...] == 1, st[...], LOW)
    v = jnp.take_along_axis(v, fine0 + jnp.bitwise_and(wide_lane, PP - 1), axis=1,
                            mode="promise_in_bounds")
    v = jnp.where(wide_lane // 16 == jnp.bitwise_and(wide_row, 7), v, 0.0)
    v = jnp.sum(v.reshape(2 * X, 8, 128), axis=1)
    for k in range(X):
        c1[k] = v[2 * k:2 * k + 2, :]

    def layer(ox, oc):
        i = ox * YC + oc
        return remote(c1.at[lax.rem(x + ox, X)], c1buf.at[i], asend.at[i], arecv.at[i],
                      {"query": lax.rem(x + ox, X), "cent": lax.rem(yc + oc, YC)})

    layers = [(ox, oc) for ox in range(X) for oc in range(YC) if ox or oc]
    layers.sort(key=lambda t: -min(t[0], X - t[0]) - min(t[1] // 2, Y - t[1] // 2))
    for t in layers:
        layer(*t).start()
    scopies = []
    for o in range(1, X):
        dst = pl.multiple_of(lax.rem(x + o, X) * 16, 16)
        scopies.append(remote(st.at[pl.ds(dst, 16)], sbuf.at[o - 1], ssend.at[o - 1],
                              srecv.at[o - 1], xpeer[o - 1]))
        scopies[-1].start()
    for t in layers:
        layer(*t).wait()
    row = iota((16, 128), 0)
    at = 16 * jnp.bitwise_and(row, 7) + jnp.bitwise_and(lane, 15)
    groups = [jnp.zeros((16, 128), F32) for _ in range(X * YC // 8)]
    for i in range(X * YC):
        v = c1buf[i] if i else c1[x]
        v = jnp.concatenate([jnp.broadcast_to(v[0:1], (8, 128)),
                             jnp.broadcast_to(v[1:2], (8, 128))], axis=0)
        v = jnp.take_along_axis(v, at, axis=1, mode="promise_in_bounds")
        groups[i // 8] = jnp.where(lane // 16 == i % 8, v, groups[i // 8])
    first = (TOPK * iota((16, 1), 0)).astype(F32)
    c2[...] = jnp.sum(top8(groups, first), axis=0, keepdims=True)
    bcopies = []
    for o in range(1, Z):
        bcopies.append(remote(c2, c2buf.at[o - 1], bsend.at[o - 1], brecv.at[o - 1], zpeer[o - 1]))
        bcopies[-1].start()

    rep = jnp.where(jnp.bitwise_and(lane, 15) == iota((16, 128), 0), 1.0, 0.0).astype(BF16)
    pos_t = jnp.dot(pos[...].astype(F32).astype(BF16), rep, preferred_element_type=F32).astype(I32)
    count = jnp.sum(jnp.where(iota((16, 16), 0) == iota((16, 16), 1), tally[...], 0),
                    axis=1, keepdims=True)
    live = jnp.bitwise_and(lane, 15) < count
    for cp in scopies:
        cp.wait()
    tot = st[pl.ds(pl.multiple_of(x * 16, 16), 16), :]
    for o in range(X - 1):
        tot = tot + sbuf[o]
    where = pos_t + jnp.where(lane < 16, 64 * (1 - c), 64 * c)
    slots = jnp.take_along_axis(tot, where, axis=1, mode="promise_in_bounds")
    slots = jnp.where(live, slots, 0.0)
    for d in sent:
        d.wait_send()
    for o in range(1, Y):
        r = table.at[:, y, c]
        remote(r, r, ysend.at[o - 1], yrecv.at[0, 0, o - 1], ypeer[o - 1]).wait_send()
    whole.wait_send()
    for cp in bcopies:
        cp.wait()
    at = TOPK * row + jnp.bitwise_and(lane, TOPK - 1)
    merged = jnp.zeros((16, 128), F32)
    for i in range(Z):
        v = jnp.broadcast_to(c2buf[i - 1] if i else c2[...], (16, 128))
        v = jnp.take_along_axis(v, at, axis=1, mode="promise_in_bounds")
        merged = jnp.where(lane // TOPK == i, v, merged)
    out[...] = jnp.where(lane < 32, slots, top8([merged], 32.0))


def fused(X, Z, YC, means, queries, shard, entry, words, amounts, pos, tally):
    PP = 64 // X
    R = 64 * PP
    CR = R // CHUNKS
    Y = YC // 2
    rows = means.shape[0] // X
    half = Z // 2
    n = queries.shape[0]
    nq = X * n
    dma = pltpu.SemaphoreType.DMA
    vm = pl.BlockSpec(memory_space=VMEM)
    hbm = pl.BlockSpec(memory_space=pltpu.HBM)
    return pl.pallas_call(
        functools.partial(kernel, X, Z, Y),
        out_shape=jax.ShapeDtypeStruct((16, 128), F32),
        in_specs=[hbm, hbm, hbm, hbm, hbm, pl.BlockSpec(memory_space=pltpu.SMEM), vm, vm],
        out_specs=vm,
        scratch_shapes=[
            VMEM((Z, Y, 2, rows, 128), BF16), VMEM((Z * YC * rows + 8, 128), F32),
            VMEM((X, n, 128), BF16), VMEM((nq, 128), BF16),
            VMEM((64, 64), I32), VMEM((64, 64), I32), VMEM((64, 64), I32),
            pltpu.SMEM((64, 64), I32), VMEM((PP, 1024), I32), VMEM((256, 1024), BF16),
            VMEM((R, 128), F32), VMEM((CR, 128), F32), VMEM((R, 128), F32),
            VMEM((X - 1, R, 128), BF16), VMEM((X - 1, R, 128), BF16),
            VMEM((CR, 128), BF16), VMEM((CR, 128), BF16),
            VMEM((128, nq), F32), VMEM((nq // 32, 128), F32), VMEM((X - 1, 16, 128), F32),
            VMEM((X, 16, 16), I32), VMEM((X, 1, 16), I32), VMEM((nq // 32, 128), I32),
            VMEM((X, 2, 128), F32), VMEM((X * YC, 2, 128), F32),
            VMEM((1, 128), F32), VMEM((Z - 1, 1, 128), F32),
            dma((5 + X,)),
            dma((2, half)), dma((2, half)), dma((2, half)), dma((2, half)),
            dma((Y - 1,)), dma((2, 2 * half + 1, Y - 1)),
            dma((X - 1,)), dma((X - 1,)), dma((1,)), dma((1,)), dma((2, X - 1)), dma((2, X - 1)),
            dma((X - 1, CHUNKS)), dma((X - 1, CHUNKS)), dma((X - 1,)), dma((X - 1,)),
            dma((X * YC,)), dma((X * YC,)), dma((Z - 1,)), dma((Z - 1,)),
        ],
        compiler_params=pltpu.CompilerParams(
            collective_id=0, has_side_effects=True, vmem_limit_bytes=60 << 20),
        name="plaid",
    )(means, queries, shard, entry, words, amounts, pos, tally)


def local(request_term_embeds, cluster_means, cluster_shard_number, cluster_entry_within,
          quantized_error_words, quantized_error_amounts, keeper_document_position,
          active_keeper_tally):
    X, Z, YC = (lax.axis_size(a) for a in ("query", "corpus", "cent"))
    out = fused(
        X, Z, YC, cluster_means, request_term_embeds.reshape(-1, 128),
        cluster_shard_number[:, :, 0], cluster_entry_within, quantized_error_words,
        quantized_error_amounts, keeper_document_position[:, 0, :],
        active_keeper_tally.reshape(1, 16))
    return out[:, None, 0:16], out[:, None, 16:32], out[:, 32:32 + TOPK]


def solution(mesh):
    return jax.shard_map(
        local,
        mesh=mesh,
        in_specs=(
            P("query", None, None),
            P(("corpus", "cent"), None),
            P(("corpus", "cent"), None, None),
            P(("corpus", "cent"), None),
            P(("corpus", "cent"), None),
            P(),
            P("query", ("corpus", "cent"), None),
            P("query", ("corpus", "cent")),
        ),
        out_specs=(
            P("query", ("corpus", "cent"), None),
            P("query", ("corpus", "cent"), None),
            P("query", None),
        ),
        check_vma=False,
    )
```

```python
import collections
import functools

import jax
import jax.numpy as jnp
from jax import lax
from jax.experimental import pallas as pl
from jax.experimental.pallas import tpu as pltpu
from jax.sharding import PartitionSpec as P

TOPK = 8
EPS = 1e-06
LOW = -1e30
MESH = pl.DeviceIdType.MESH
F32 = jnp.float32
BF16 = jnp.bfloat16
I32 = jnp.int32
VMEM = pltpu.VMEM
NT = (((1,), (1,)), ((), ()))
CHUNKS = 8


def iota(shape, axis):
    return lax.broadcasted_iota(I32, shape, axis)


def remote(src, dst, s, r, d):
    return pltpu.make_async_remote_copy(
        src_ref=src, dst_ref=dst, send_sem=s, recv_sem=r, device_id=d, device_id_type=MESH)


def top8(vs, base):
    lane = iota(vs[0].shape, 1).astype(F32)
    first = jnp.zeros((vs[0].shape[0], 1), F32) + base
    cum = first
    out = jnp.zeros(vs[0].shape, F32)
    for _ in range(TOPK):
        m = jnp.max(functools.reduce(jnp.maximum, vs), axis=1, keepdims=True)
        out = jnp.where(lane >= cum, m, out)
        equal = [v == m for v in vs]
        seen = functools.reduce(jnp.add, [jnp.where(e, 1.0, 0.0) for e in equal])
        cum = cum + jnp.sum(seen, axis=1, keepdims=True)
        vs = [jnp.where(e, -3e38, v) for e, v in zip(equal, vs)]
    return jnp.where((lane >= first) & (lane < first + TOPK), out, 0.0)


def kernel(X, Z, Y, means, qin, shard, entry, words, amounts, pos, tally, out,
           table, wide, qall, qn, shard_v, entry_v, idx_v, idx, wbuf, spread, res, got, own,
           part, rbuf, dc, df, mp, st, sbuf, pos_all, tal_all, keep, c1, c1buf, c2, c2buf,
           lsem, rsend, rrecv, lsend, lrecv, ysend, yrecv, qsend, qrecv, psend, precv, tsend, trecv,
           xsend, xrecv, ssend, srecv, asend, arecv, bsend, brecv):
    x = lax.axis_index("query")
    z = lax.axis_index("corpus")
    yc = lax.axis_index("cent")
    YC = 2 * Y
    y, c = yc // 2, lax.rem(yc, 2)
    PP = 64 // X
    rows = table.shape[3]
    hr = rows // 2
    half = Z // 2
    total = Z * YC * rows
    R = 64 * PP
    CR = R // CHUNKS

    mine = means.at[pl.ds(x * rows, rows)]
    locals_ = [
        pltpu.make_async_copy(mine, table.at[z, y, c], lsem.at[0]),
        pltpu.make_async_copy(qin, qall.at[x], lsem.at[1]),
        pltpu.make_async_copy(shard, shard_v, lsem.at[2]),
        pltpu.make_async_copy(entry, entry_v, lsem.at[3]),
        pltpu.make_async_copy(words.at[pl.ds(x * PP, PP)], wbuf, lsem.at[4]),
    ]
    for d in locals_:
        d.start()

    zdev = {(k, r): {"corpus": lax.rem(z + (k if r else Z - k), Z)} for k in (1, 2) for r in (True, False)}
    mate = {"cent": y * 2 + 1 - c}
    ypeer = [{"cent": lax.rem(y + o, Y) * 2 + c} for o in range(1, Y)]
    xpeer = [{"query": lax.rem(x + o, X)} for o in range(1, X)]
    zpeer = [{"corpus": lax.rem(z + o, Z)} for o in range(1, Z)]
    bar = pltpu.get_barrier_semaphore()
    near = list(zdev.values()) + [mate] + ypeer + xpeer
    for d in near:
        pl.semaphore_signal(bar, inc=1, device_id=d, device_id_type=MESH)
    pl.semaphore_wait(bar, len(near))

    def origin(s, right):
        return lax.rem(z + Z - s, Z) if right else lax.rem(z + s, Z)

    def ref(zo, yo, h):
        return table.at[zo, yo, c, pl.ds(h * hr, hr)]

    def last(h, right):
        return half if (h == 0) == right else half - 1

    def ring(h, s, right, hop):
        r = ref(origin(s, right), y, h)
        return remote(r, r, (rsend if right else lsend).at[h, s + hop - 1],
                      (rrecv if right else lrecv).at[h, s + hop - 1], zdev[hop, right])

    def slot(s, right):
        return s if right else half + s

    def ycopy(h, s, right, yo, to, tag):
        r = ref(origin(s, right), yo, h)
        return remote(r, r, ysend.at[tag - 1], yrecv.at[h, slot(s, right), tag - 1], ypeer[to - 1])

    def widen(zo, yo, h, cc, n):
        base = pl.multiple_of(((zo * Y + yo) * 2 + cc) * rows + h * hr, hr)
        wide[pl.ds(base, n), :] = table[zo, yo, cc, pl.ds(h * hr, n), :].astype(F32)

    def to_mate(zo, yo, h):
        r = ref(zo, yo, h)
        remote(r, r, psend.at[0], precv.at[0], mate).start()

    sent = []
    pending, relayed = collections.deque(), collections.deque()

    def forward(h, s, right, hop):
        if s + hop <= last(h, right):
            d = ring(h, s, right, hop)
            d.start()
            sent.append(d)

    def along_y(h, s, right):
        for o in (1, Y - 1):
            ycopy(h, s, right, y, o, o).start()
        pending.append((h, s, right))

    def collect(upto):
        while pending and pending[0][1] <= upto:
            h, s, right = pending.popleft()
            for o in (1, Y - 1):
                ycopy(h, s, right, lax.rem(y + Y - o, Y), o, o).wait_recv()
                if (h == 0) == (o == 1):
                    ycopy(h, s, right, lax.rem(y + Y - o, Y), o, 2).start()
            for o in (1, Y - 1):
                to_mate(origin(s, right), lax.rem(y + Y - o, Y), h)
            for o in (1, Y - 1):
                widen(origin(s, right), lax.rem(y + Y - o, Y), h, c, hr)
            relayed.append((h, s, right))

    def collect_relayed(upto):
        while relayed and relayed[0][1] <= upto:
            h, s, right = relayed.popleft()
            yo = lax.rem(y + 2, Y)
            ycopy(h, s, right, yo, 1, 2).wait_recv()
            to_mate(origin(s, right), yo, h)
            widen(origin(s, right), yo, h, c, hr)

    def make_index():
        locals_[2].wait()
        locals_[3].wait()
        e = entry_v[...]
        idx_v[...] = jnp.where(e // rows == x, shard_v[...] * rows + lax.rem(e, rows), total)
        for o in range(X):
            src = idx_v.at[pl.ds(pl.multiple_of(lax.rem(x + o, X) * PP, PP), PP)]
            pltpu.make_async_copy(src, idx.at[pl.ds(o * PP, PP)], lsem.at[5 + o]).start()
        wide[pl.ds(total, 8), :] = jnp.zeros((8, 128), F32)

    def make_spread():
        col = iota((256, 1024), 1)
        d = jnp.bitwise_and(col, 127)
        want = (col // 128) * 16 + d // 8 + jnp.where(jnp.bitwise_and(d, 4) != 0, 128, 0)
        spread[...] = jnp.where(iota((256, 1024), 0) == want, 1.0, 0.0).astype(BF16)

    def decode():
        locals_[4].wait()
        w = jnp.concatenate([wbuf[:, 128 * g:128 * (g + 1)] for g in range(8)], axis=0)
        lo = jnp.bitwise_and(w, 255).astype(F32).astype(BF16)
        hi = jnp.bitwise_and(jnp.right_shift(w, 8), 255).astype(F32).astype(BF16)
        code = jnp.dot(jnp.concatenate([lo, hi], axis=1), spread[...],
                       preferred_element_type=F32).astype(I32)
        bit = jnp.left_shift(1, 2 * jnp.bitwise_and(iota(code.shape, 1), 3))
        b0 = jnp.bitwise_and(code, bit) != 0
        b1 = jnp.bitwise_and(code, 2 * bit) != 0
        r = jnp.where(b1, jnp.where(b0, amounts[3], amounts[2]), jnp.where(b0, amounts[1], amounts[0]))
        for t in range(8):
            res[pl.ds(t * 8 * PP, 8 * PP), :] = r[:, 128 * t:128 * (t + 1)]

    def normalize(k):
        q = qall[k].astype(F32)
        n = q.shape[0]
        qn[pl.ds(pl.multiple_of(k * n, n), n), :] = (
            q * lax.rsqrt(jnp.sum(q * q, axis=1, keepdims=True) + EPS)).astype(BF16)

    def normalize_own():
        locals_[1].wait()
        normalize(x)

    def normalize_peer(o):
        remote(qin, qall.at[x], qsend.at[o - 1], qrecv.at[o - 1], xpeer[o - 1]).wait()
        normalize(lax.rem(x + X - o, X))

    lane = iota((16, 128), 1)
    fine0 = 64 * c + PP * x
    coarse0 = 64 * (1 - c) + PP * x

    def keep_rows(k):
        p = pos_all[k]
        count = jnp.sum(jnp.where(iota((16, 16), 0) == iota((16, 16), 1), tal_all[k], 0),
                        axis=1, keepdims=True)
        p = jnp.where(iota((16, 16), 1) < count, p, -1000)
        kept = jnp.zeros((16, 128), I32)
        for j in range(16):
            kept = jnp.where(p[:, j:j + 1] - PP * x == lane - fine0, 1, kept)
        kept = jnp.where((lane >= fine0) & (lane < fine0 + PP), kept, 2)
        keep[pl.ds(pl.multiple_of(k * 16, 16), 16), :] = kept

    def keep_peer(o):
        remote(pos, pos_all.at[x], tsend.at[0, o - 1], trecv.at[0, o - 1], xpeer[o - 1]).wait()
        remote(tally, tal_all.at[x], tsend.at[1, o - 1], trecv.at[1, o - 1], xpeer[o - 1]).wait()
        keep_rows(lax.rem(x + X - o, X))

    def keep_own():
        pos_all[x] = pos[...]
        tal_all[x] = tally[...]
        keep_rows(x)

    def keep_all():
        keep_own()
        for o in range(1, X):
            keep_peer(o)

    work = collections.deque([make_index, make_spread, keep_all, decode, normalize_own] +
                             [functools.partial(normalize_peer, o) for o in range(1, X)])

    locals_[0].wait()
    for hop in (1, 2):
        for h in range(2):
            forward(h, 0, True, hop)
            forward(h, 0, False, hop)
    for h in range(2):
        along_y(h, 0, True)
    for o in range(1, X):
        remote(pos, pos_all.at[x], tsend.at[0, o - 1], trecv.at[0, o - 1], xpeer[o - 1]).start()
        remote(tally, tal_all.at[x], tsend.at[1, o - 1], trecv.at[1, o - 1], xpeer[o - 1]).start()
        remote(qin, qall.at[x], qsend.at[o - 1], qrecv.at[o - 1], xpeer[o - 1]).start()
    for h in range(2):
        to_mate(z, y, h)
    widen(z, y, 0, c, rows)
    work.popleft()()
    for s in range(1, half + 1):
        here = [(h, right) for h in range(2) for right in (True, False) if s <= last(h, right)]
        for h, right in here:
            r = ref(origin(s, right), y, h)
            remote(r, r, (rsend if right else lsend).at[h, s - 1],
                   (rrecv if right else lrecv).at[h, s - 1], zdev[1, right]).wait_recv()
            forward(h, s, right, 2)
        for h, right in here:
            along_y(h, s, right)
        for h, right in here:
            to_mate(origin(s, right), y, h)
        for h, right in here:
            widen(origin(s, right), y, h, c, hr)
        collect(s - 3)
        collect_relayed(s - 5)
        if work:
            work.popleft()()
    while work:
        work.popleft()()
    collect(half)
    collect_relayed(half)
    whole = remote(table.at[:, :, c], table.at[:, :, 1 - c], psend.at[0], precv.at[0], mate)
    whole.wait_recv()

    def widen_mate(i, carry):
        for yo in range(Y):
            widen(i, yo, 0, 1 - c, rows)
        return carry

    lax.fori_loop(0, Z, widen_mate, 0)
    for o in range(X):
        pltpu.make_async_copy(idx_v.at[pl.ds(0, PP)], idx.at[pl.ds(o * PP, PP)], lsem.at[5 + o]).wait()

    tc = 8 // CHUNKS

    def xcopy(o, ch):
        piece = pl.ds(ch * CR, CR)
        return remote(part.at[o - 1, piece], rbuf.at[o - 1, piece], xsend.at[o - 1, ch],
                      xrecv.at[o - 1, ch], xpeer[o - 1])

    order = [o for o in (2, 1, 3) if o < X] + [o for o in range(4, X)]
    for ch in range(CHUNKS):
        for o in order + [0]:
            def pick(g, carry, o=o, ch=ch):
                for t in range(tc):
                    k = 8 * g + ch * tc + t
                    picked = [wide[pl.ds(idx[o * PP + j, k], 1), :] for j in range(PP)]
                    base = pl.multiple_of(g * PP + t * 8 * PP, PP)
                    for j in range(PP):
                        if o:
                            got[pl.ds(base + j, 1), :] = picked[j]
                        else:
                            own[pl.ds(base + ch * CR + j, 1), :] = picked[j]
                return carry

            lax.fori_loop(0, 8, pick, 0)
            if o:
                part[o - 1, ch * CR:(ch + 1) * CR, :] = got[...].astype(BF16)
                xcopy(o, ch).start()

    mp[...] = jnp.zeros_like(mp)
    nq = qn.shape[0]
    blk = 256
    for ch in range(CHUNKS):
        a, b = ch * CR, (ch + 1) * CR
        v = own[a:b, :]
        for o in order:
            xcopy(o, ch).wait()
            v = v + rbuf[o - 1, a:b, :].astype(F32)
        dc[...] = v.astype(BF16)
        e = v + res[a:b, :]
        df[...] = (e * lax.rsqrt(jnp.sum(e * e, axis=1, keepdims=True) + EPS)).astype(BF16)
        for which, docs in ((0, dc), (1, df)):
            row = pl.multiple_of(fine0 if which else coarse0, PP)
            for n in range(nq // blk):
                sim = lax.dot_general(docs[...], qn[n * blk:(n + 1) * blk, :], NT,
                                      preferred_element_type=F32)
                m = jnp.max(sim.reshape(CR // PP, PP, blk), axis=0)
                if ch:
                    m = jnp.maximum(m, mp[pl.ds(row, PP), n * blk:(n + 1) * blk])
                mp[pl.ds(row, PP), n * blk:(n + 1) * blk] = m
    ones = jnp.where(iota((nq // 32, nq), 1) // 32 == iota((nq // 32, nq), 0), 1.0, 0.0)
    st[...] = lax.dot_general(ones, mp[...], NT, precision=lax.Precision.HIGHEST,
                              preferred_element_type=F32)

    wide_lane, wide_row = iota(st.shape, 1), iota(st.shape, 0)
    v = jnp.where(keep[...] == 1, st[...], LOW)
    v = jnp.take_along_axis(v, fine0 + jnp.bitwise_and(wide_lane, PP - 1), axis=1,
                            mode="promise_in_bounds")
    v = jnp.where(wide_lane // 16 == jnp.bitwise_and(wide_row, 7), v, 0.0)
    v = jnp.sum(v.reshape(2 * X, 8, 128), axis=1)
    for k in range(X):
        c1[k] = v[2 * k:2 * k + 2, :]

    def layer(ox, oc):
        i = ox * YC + oc
        return remote(c1.at[lax.rem(x + ox, X)], c1buf.at[i], asend.at[i], arecv.at[i],
                      {"query": lax.rem(x + ox, X), "cent": lax.rem(yc + oc, YC)})

    layers = [(ox, oc) for ox in range(X) for oc in range(YC) if ox or oc]
    layers.sort(key=lambda t: -min(t[0], X - t[0]) - min(t[1] // 2, Y - t[1] // 2))
    for t in layers:
        layer(*t).start()
    scopies = []
    for o in range(1, X):
        dst = pl.multiple_of(lax.rem(x + o, X) * 16, 16)
        scopies.append(remote(st.at[pl.ds(dst, 16)], sbuf.at[o - 1], ssend.at[o - 1],
                              srecv.at[o - 1], xpeer[o - 1]))
        scopies[-1].start()
    for t in layers:
        layer(*t).wait()
    row = iota((16, 128), 0)
    at = 16 * jnp.bitwise_and(row, 7) + jnp.bitwise_and(lane, 15)
    groups = [jnp.zeros((16, 128), F32) for _ in range(X * YC // 8)]
    for i in range(X * YC):
        v = c1buf[i] if i else c1[x]
        v = jnp.concatenate([jnp.broadcast_to(v[0:1], (8, 128)),
                             jnp.broadcast_to(v[1:2], (8, 128))], axis=0)
        v = jnp.take_along_axis(v, at, axis=1, mode="promise_in_bounds")
        groups[i // 8] = jnp.where(lane // 16 == i % 8, v, groups[i // 8])
    first = (TOPK * iota((16, 1), 0)).astype(F32)
    c2[...] = jnp.sum(top8(groups, first), axis=0, keepdims=True)
    bcopies = []
    for o in range(1, Z):
        bcopies.append(remote(c2, c2buf.at[o - 1], bsend.at[o - 1], brecv.at[o - 1], zpeer[o - 1]))
        bcopies[-1].start()

    rep = jnp.where(jnp.bitwise_and(lane, 15) == iota((16, 128), 0), 1.0, 0.0).astype(BF16)
    pos_t = jnp.dot(pos[...].astype(F32).astype(BF16), rep, preferred_element_type=F32).astype(I32)
    count = jnp.sum(jnp.where(iota((16, 16), 0) == iota((16, 16), 1), tally[...], 0),
                    axis=1, keepdims=True)
    live = jnp.bitwise_and(lane, 15) < count
    for cp in scopies:
        cp.wait()
    tot = st[pl.ds(pl.multiple_of(x * 16, 16), 16), :]
    for o in range(X - 1):
        tot = tot + sbuf[o]
    where = pos_t + jnp.where(lane < 16, 64 * (1 - c), 64 * c)
    slots = jnp.take_along_axis(tot, where, axis=1, mode="promise_in_bounds")
    slots = jnp.where(live, slots, 0.0)
    for d in sent:
        d.wait_send()
    for o in range(1, Y):
        r = table.at[:, y, c]
        remote(r, r, ysend.at[o - 1], yrecv.at[0, 0, o - 1], ypeer[o - 1]).wait_send()
    whole.wait_send()
    for cp in bcopies:
        cp.wait()
    at = TOPK * row + jnp.bitwise_and(lane, TOPK - 1)
    merged = jnp.zeros((16, 128), F32)
    for i in range(Z):
        v = jnp.broadcast_to(c2buf[i - 1] if i else c2[...], (16, 128))
        v = jnp.take_along_axis(v, at, axis=1, mode="promise_in_bounds")
        merged = jnp.where(lane // TOPK == i, v, merged)
    out[...] = jnp.where(lane < 32, slots, top8([merged], 32.0))


def fused(X, Z, YC, means, queries, shard, entry, words, amounts, pos, tally):
    PP = 64 // X
    R = 64 * PP
    CR = R // CHUNKS
    Y = YC // 2
    rows = means.shape[0] // X
    half = Z // 2
    n = queries.shape[0]
    nq = X * n
    dma = pltpu.SemaphoreType.DMA
    vm = pl.BlockSpec(memory_space=VMEM)
    hbm = pl.BlockSpec(memory_space=pltpu.HBM)
    return pl.pallas_call(
        functools.partial(kernel, X, Z, Y),
        out_shape=jax.ShapeDtypeStruct((16, 128), F32),
        in_specs=[hbm, hbm, hbm, hbm, hbm, pl.BlockSpec(memory_space=pltpu.SMEM), vm, vm],
        out_specs=vm,
        scratch_shapes=[
            VMEM((Z, Y, 2, rows, 128), BF16), VMEM((Z * YC * rows + 8, 128), F32),
            VMEM((X, n, 128), BF16), VMEM((nq, 128), BF16),
            VMEM((64, 64), I32), VMEM((64, 64), I32), VMEM((64, 64), I32),
            pltpu.SMEM((64, 64), I32), VMEM((PP, 1024), I32), VMEM((256, 1024), BF16),
            VMEM((R, 128), F32), VMEM((CR, 128), F32), VMEM((R, 128), F32),
            VMEM((X - 1, R, 128), BF16), VMEM((X - 1, R, 128), BF16),
            VMEM((CR, 128), BF16), VMEM((CR, 128), BF16),
            VMEM((128, nq), F32), VMEM((nq // 32, 128), F32), VMEM((X - 1, 16, 128), F32),
            VMEM((X, 16, 16), I32), VMEM((X, 1, 16), I32), VMEM((nq // 32, 128), I32),
            VMEM((X, 2, 128), F32), VMEM((X * YC, 2, 128), F32),
            VMEM((1, 128), F32), VMEM((Z - 1, 1, 128), F32),
            dma((5 + X,)),
            dma((2, half)), dma((2, half)), dma((2, half)), dma((2, half)),
            dma((Y - 1,)), dma((2, 2 * half + 1, Y - 1)),
            dma((X - 1,)), dma((X - 1,)), dma((1,)), dma((1,)), dma((2, X - 1)), dma((2, X - 1)),
            dma((X - 1, CHUNKS)), dma((X - 1, CHUNKS)), dma((X - 1,)), dma((X - 1,)),
            dma((X * YC,)), dma((X * YC,)), dma((Z - 1,)), dma((Z - 1,)),
        ],
        compiler_params=pltpu.CompilerParams(
            collective_id=0, has_side_effects=True, vmem_limit_bytes=60 << 20),
        name="plaid",
    )(means, queries, shard, entry, words, amounts, pos, tally)


def local(request_term_embeds, cluster_means, cluster_shard_number, cluster_entry_within,
          quantized_error_words, quantized_error_amounts, keeper_document_position,
          active_keeper_tally):
    X, Z, YC = (lax.axis_size(a) for a in ("query", "corpus", "cent"))
    out = fused(
        X, Z, YC, cluster_means, request_term_embeds.reshape(-1, 128),
        cluster_shard_number[:, :, 0], cluster_entry_within, quantized_error_words,
        quantized_error_amounts, keeper_document_position[:, 0, :],
        active_keeper_tally.reshape(1, 16))
    return out[:, None, 0:16], out[:, None, 16:32], out[:, 32:32 + TOPK]


def solution(mesh):
    return jax.shard_map(
        local,
        mesh=mesh,
        in_specs=(
            P("query", None, None),
            P(("corpus", "cent"), None),
            P(("corpus", "cent"), None, None),
            P(("corpus", "cent"), None),
            P(("corpus", "cent"), None),
            P(),
            P("query", ("corpus", "cent"), None),
            P("query", ("corpus", "cent")),
        ),
        out_specs=(
            P("query", ("corpus", "cent"), None),
            P("query", ("corpus", "cent"), None),
            P("query", None),
        ),
        check_vma=False,
    )
```
